128 devices in a mesh: row: 8 (over y, core), col: 16 (over z, x).
Axes of the slice: x: 4, y: 4, z: 4, core: 2. Of those that a mesh axis runs over, the one named last changes fastest.
Arguments:
- y_blocks: bfloat16 [512, 16, 128, 128], P(('row', 'col')), may hold values from -0.3 to 1.3
- z_blocks: bfloat16 [512, 16, 128, 128], P(('row', 'col')), may hold values from -0.3 to 1.3
- pattern: int32 [512, 16], replicated, may hold values from 0 to 511, as said below
Outputs:
- y_next: bfloat16 [512, 16, 128, 128], P(('row', 'col'))
- z_next: bfloat16 [512, 16, 128, 128], P(('row', 'col'))
The draws below stay inside these ranges and needn't reach their ends.
Inputs may be any that keep to these rules, and one draw needn't show every extreme that they name: `pattern`: block row i = (16 x + y) * 4 + z belongs to the domain (x, y, z) of a periodic grid of 8 x 16 x 4 domains. It lists 16 distinct block columns, among them i itself; every column is the block row of a domain ((x + a) mod 8, (y + b) mod 16, (z + c) mod 4) with (a, b) one of (0, 0), (1, 0), (-1, 0), (0, 1), (0, -1) and -1 <= c <= 2.
All inputs are finite; a program needn't handle non-finite values.
Results may differ from the reference program's by a relative error of at most 0.0052.
Values may be sent and summed in bfloat16 or wider, within the bound.
A program may use at most 192 MiB of HBM per device.

```python
import jax
import jax.numpy as jnp
import numpy as np
from jax import lax

BS = 128
K = 16
RB = 4
GX = 8
GY = 16
NB = 512


def candidate_table():
    entries = []
    for shift_pair in ((0, 0), (-1, 0), (1, 0), (0, -1), (0, 1)):
        for shift_z in (-1, 0, 1, 2):
            if shift_pair[0] != 0 or shift_pair[1] != 0 or shift_z != 0:
                entries.append([shift_pair[0], shift_pair[1], shift_z])
    return np.array(entries, dtype=np.int32)


def shared_pattern(key):
    base = jax.random.fold_in(key, 7)
    table = candidate_table()
    candidate_count = table.shape[0]
    scores = jax.random.randint(base, (NB, candidate_count), 0, 1 << 20) * candidate_count + jnp.arange(candidate_count, dtype=jnp.int32)[None, :]
    ranking = jnp.argsort(scores, axis=1)[:, :K - 1]
    zero_lane = jnp.zeros((NB, 1), jnp.int32)
    shift_x = jnp.concatenate([zero_lane, jnp.take(jnp.asarray(table[:, 0]), ranking)], axis=1)
    shift_y = jnp.concatenate([zero_lane, jnp.take(jnp.asarray(table[:, 1]), ranking)], axis=1)
    shift_z = jnp.concatenate([zero_lane, jnp.take(jnp.asarray(table[:, 2]), ranking)], axis=1)
    mixing = jax.random.randint(jax.random.fold_in(base, 1), (NB, K), 0, 1 << 20) * K + jnp.arange(K, dtype=jnp.int32)[None, :]
    shuffle = jnp.argsort(mixing, axis=1)
    shift_x = jnp.take_along_axis(shift_x, shuffle, axis=1)
    shift_y = jnp.take_along_axis(shift_y, shuffle, axis=1)
    shift_z = jnp.take_along_axis(shift_z, shuffle, axis=1)
    rows_all = jnp.arange(NB, dtype=jnp.int32)
    row_z = jnp.mod(rows_all, RB)[:, None]
    row_y = jnp.mod(rows_all // RB, GY)[:, None]
    row_x = (rows_all // (RB * GY))[:, None]
    column = (jnp.mod(row_x + shift_x, GX) * GY + jnp.mod(row_y + shift_y, GY)) * RB + jnp.mod(row_z + shift_z, RB)
    return column.astype(jnp.int32)


def noisy_blocks(key, salt):
    noise_key = jax.random.fold_in(key, salt)
    values = 0.05 * jax.random.truncated_normal(noise_key, -5.8, 5.8, (NB, K, BS, BS), jnp.float32)
    pattern = shared_pattern(key)
    diagonal = pattern == jnp.arange(NB, dtype=jnp.int32)[:, None]
    identity = jnp.eye(BS, dtype=jnp.float32)
    values = values + jnp.where(diagonal[:, :, None, None], identity, jnp.float32(0.0))
    return values.astype(jnp.bfloat16)


def draw_y_blocks(key, part):
    return noisy_blocks(key, 11)


def draw_z_blocks(key, part):
    return noisy_blocks(key, 13)


def draw_pattern(key, part):
    return shared_pattern(key)


def setup_inputs(seed: int = 0) -> dict:
    seeds = jax.random.split(jax.random.key(seed), 4)
    return {
        "y_blocks": draw_y_blocks(jax.random.fold_in(seeds[3], 71), 0),
        "z_blocks": draw_z_blocks(jax.random.fold_in(seeds[3], 71), 0),
        "pattern": draw_pattern(jax.random.fold_in(seeds[3], 71), 0),
    }


def sparse_product(factor, other, pattern):
    lane_ids = jnp.arange(pattern.shape[1], dtype=jnp.int32)

    def one_row(inputs):
        factor_row, row_cols = inputs
        partner = jnp.take(other, row_cols, axis=0)
        partner_cols = jnp.take(pattern, row_cols, axis=0)
        matches = partner_cols[:, :, None] == row_cols[None, None, :]
        position = jnp.sum(jnp.where(matches, lane_ids[None, :, None], 0), axis=1).astype(jnp.int32)
        present = jnp.any(matches, axis=1)
        chosen = jnp.take_along_axis(partner, position[:, :, None, None], axis=1)
        chosen = jnp.where(present[:, :, None, None], chosen, jnp.zeros_like(chosen))
        return jnp.einsum("kab,kmbc->mac", factor_row.astype(jnp.float32), chosen.astype(jnp.float32))

    return lax.map(one_row, (factor, pattern), batch_size=16)


def reference(y_blocks, z_blocks, pattern):
    product = sparse_product(z_blocks, y_blocks, pattern)
    diagonal = pattern == jnp.arange(pattern.shape[0], dtype=jnp.int32)[:, None]
    identity = jnp.eye(y_blocks.shape[2], dtype=jnp.float32)
    t_blocks = (1.5 * jnp.where(diagonal[:, :, None, None], identity, jnp.float32(0.0)) - 0.5 * product).astype(jnp.bfloat16)
    y_next = sparse_product(y_blocks, t_blocks, pattern).astype(jnp.bfloat16)
    z_next = sparse_product(t_blocks, z_blocks, pattern).astype(jnp.bfloat16)
    return y_next, z_next
```

```python
import functools

import jax
import jax.numpy as jnp
from jax import lax
from jax.experimental import pallas as pl
from jax.experimental.pallas import tpu as pltpu
from jax.sharding import PartitionSpec as P

MESH = pl.DeviceIdType.MESH
Y_EDGE, Y_DIAG, Z_EDGE, Z_DIAG, T_DIAG = range(5)
SEND_ORDER = (2, 3, 0, 1)


def step_kernel(
    layout,
    y_hbm, z_hbm, pat_hbm,
    y_out, z_out,
    y_raw, z_raw, pat, keep, tab_v, tab,
    y_own, z_own, t_own, got, t_near, y_part, acc, y_acc, z_acc,
    y_dense, z_dense,
    in_sem, send_sem, recv_sem,
):
    row_count, col_count, rows, bs = layout
    lanes = pat.shape[1]
    me_r, me_c = lax.axis_index("row"), lax.axis_index("col")

    def neighbour(d):
        if isinstance(d, int):
            step_r = (-1, 1, 0, 0)[d]
            step_c = (0, 0, -1, 1)[d]
        else:
            step_r = jnp.where(d < 2, 2 * d - 1, 0)
            step_c = jnp.where(d < 2, 0, 2 * d - 5)
        return (
            lax.rem(me_r + step_r + row_count, row_count),
            lax.rem(me_c + step_c + col_count, col_count),
        )

    copies = [
        pltpu.make_async_copy(pat_hbm, pat, in_sem.at[0]),
        pltpu.make_async_copy(y_hbm, y_raw.at[:, 0:lanes], in_sem.at[1]),
        pltpu.make_async_copy(z_hbm, z_raw.at[:, 0:lanes], in_sem.at[2]),
    ]
    for copy in copies:
        copy.start()
    barrier = pltpu.get_barrier_semaphore()
    for d in range(4):
        pl.semaphore_signal(barrier, 1, device_id=neighbour(d), device_id_type=MESH)

    for raw in (y_raw, z_raw):
        for i in range(rows):
            raw[i, lanes] = jnp.zeros((bs, bs), raw.dtype)
    copies[0].wait()
    lane = lax.broadcasted_iota(jnp.int32, (rows, lanes), 1)
    wide = lax.broadcasted_iota(jnp.int32, (rows, 128), 1)

    def base(place):
        return (place[0] * col_count + place[1]) * rows

    def pat_rows(start):
        return pat[pl.ds(pl.multiple_of(start, rows), rows), :]

    bases = [base((me_r, me_c))] + [base(neighbour(d)) for d in range(4)]
    own = pat_rows(bases[0])
    where_own = jnp.zeros((rows, 128), jnp.int32)
    back = jnp.zeros((rows, lanes), jnp.int32)
    for u in range(5):
        for c in range(rows):
            match = own == bases[u] + c
            at = jnp.max(jnp.where(match, lane, -1), axis=1, keepdims=True)
            keep[u, :, c * bs : (c + 1) * bs] = jnp.broadcast_to(at, (rows, bs))
            at = jnp.where(at < 0, lanes, at)
            where_own = jnp.where(wide == u * rows + c, at, where_own)
            back = jnp.where(match, u * rows + c, back)
    for d in range(4):
        near = pat_rows(bases[1 + d])
        for c in range(rows):
            match = near == bases[0] + c
            at = jnp.max(jnp.where(match, lane, -1), axis=1, keepdims=True)
            keep[5 + d, :, c * bs : (c + 1) * bs] = jnp.broadcast_to(at, (rows, bs))
    tab_v[...] = jnp.zeros_like(tab_v)
    tab_v[0:rows, :] = where_own
    tab_v[8 : 8 + rows, 0:lanes] = back
    to_scalar = pltpu.make_async_copy(tab_v, tab, in_sem.at[3])
    to_scalar.start()
    to_scalar.wait()

    def densify(raw, dense, u):
        def one(i, _):
            at_rows = pl.ds(pl.multiple_of(i * bs, bs), bs)
            for c in range(rows):
                dense[u, at_rows, c * bs : (c + 1) * bs] = raw[i, tab[i, u * rows + c]]
            return 0

        lax.fori_loop(0, rows, one, 0)

    def transfer(kind, d, source):
        back_d = d ^ 1 if isinstance(d, int) else d + 1 - 2 * lax.rem(d, 2)
        return pltpu.make_async_remote_copy(
            src_ref=source,
            dst_ref=got.at[kind, back_d],
            send_sem=send_sem.at[kind, d],
            recv_sem=recv_sem.at[kind, back_d],
            device_id=neighbour(d),
            device_id_type=MESH,
        )

    def arrival(kind, d):
        return pltpu.make_async_remote_copy(
            src_ref=got.at[kind, d],
            dst_ref=got.at[kind, d],
            send_sem=send_sem.at[kind, d],
            recv_sem=recv_sem.at[kind, d],
            device_id=neighbour(d),
            device_id_type=MESH,
        )

    sends = []

    def send(kind, d, source):
        copy = transfer(kind, d, source)
        copy.start()
        sends.append(copy)

    copies[1].wait()
    for d in SEND_ORDER:
        densify(y_raw, y_own, 1 + d)
    pl.semaphore_wait(barrier, 4)
    for d in SEND_ORDER:
        send(Y_EDGE, d, y_own.at[1 + d])
    densify(y_raw, y_own, 0)
    for d in SEND_ORDER:
        send(Y_DIAG, d, y_own.at[0])
    copies[2].wait()
    for d in SEND_ORDER:
        densify(z_raw, z_own, 1 + d)
    for d in SEND_ORDER:
        send(Z_EDGE, d, z_own.at[1 + d])
    densify(z_raw, z_own, 0)
    for d in SEND_ORDER:
        send(Z_DIAG, d, z_own.at[0])

    def dot(a, b):
        return jnp.dot(a, b, preferred_element_type=jnp.float32)

    def store_t(target, u, diagonal):
        def one(i, _):
            at_rows = pl.ds(pl.multiple_of(i * bs, bs), bs)
            value = -0.5 * acc[at_rows, :]
            if diagonal:
                r = lax.broadcasted_iota(jnp.int32, value.shape, 0) + i * bs
                s = lax.broadcasted_iota(jnp.int32, value.shape, 1)
                value = jnp.where(r == s, 1.5 + value, value)
            present = jnp.broadcast_to(keep[u, pl.ds(i, 1), :], value.shape) >= 0
            target[at_rows, :] = jnp.where(present, value, 0.0).astype(jnp.bfloat16)
            return 0

        lax.fori_loop(0, rows, one, 0)

    def store_blocks(blocks, u, source):
        def one(i, _):
            at_rows = pl.ds(pl.multiple_of(i * bs, bs), bs)
            for c in range(rows):
                block = source[at_rows, c * bs : (c + 1) * bs]
                blocks[u * rows + c, i] = block.astype(jnp.bfloat16)
            return 0

        lax.fori_loop(0, rows, one, 0)

    acc[...] = dot(z_own[0], y_own[0])

    def add_edge(d, _):
        arrival(Y_EDGE, d).wait_recv()
        acc[...] += dot(z_own[1 + d], got[Y_EDGE, d])
        return 0

    lax.fori_loop(0, 4, add_edge, 0)
    store_t(t_own.at[0], 0, True)
    for d in SEND_ORDER:
        send(T_DIAG, d, t_own.at[0])
    y_acc[...] = dot(y_own[0], t_own[0])
    z_acc[...] = dot(t_own[0], z_own[0])

    def t_edge(d, _):
        acc[...] = dot(z_own[0], y_own[1 + d])
        arrival(Y_DIAG, d).wait_recv()
        acc[...] += dot(z_own[1 + d], got[Y_DIAG, d])
        store_t(t_own.at[1 + d], 1 + d, False)
        y_part[d] = dot(y_own[0], t_own[1 + d])
        return 0

    lax.fori_loop(0, 4, t_edge, 0)

    def z_step(d, _):
        arrival(Z_EDGE, d).wait_recv()
        acc[...] = dot(got[Z_EDGE, d], y_own[0])
        z_acc[...] += dot(t_own[1 + d], got[Z_EDGE, d])
        arrival(Z_DIAG, d).wait_recv()
        acc[...] += dot(got[Z_DIAG, d], got[Y_EDGE, d])
        store_t(t_near, 5 + d, False)
        y_acc[...] += dot(y_own[1 + d], t_near[...])
        acc[...] = dot(t_own[0], z_own[1 + d])
        acc[...] += dot(t_own[1 + d], got[Z_DIAG, d])
        store_blocks(z_dense, 1 + d, acc)
        return 0

    lax.fori_loop(0, 4, z_step, 0)
    store_blocks(z_dense, 0, z_acc)
    store_blocks(y_dense, 0, y_acc)

    def gather(blocks, out):
        def one(i, _):
            for m in range(lanes):
                out[i, m] = blocks[tab[8 + i, m], i]
            return 0

        lax.fori_loop(0, rows, one, 0)

    gather(z_dense, z_out)

    def y_step(d, _):
        arrival(T_DIAG, d).wait_recv()
        acc[...] = y_part[d] + dot(y_own[1 + d], got[T_DIAG, d])
        store_blocks(y_dense, 1 + d, acc)
        return 0

    lax.fori_loop(0, 4, y_step, 0)
    gather(y_dense, y_out)
    for copy in sends:
        copy.wait_send()


def on_device(row_count, col_count, y_blocks, z_blocks, pattern):
    rows, lanes, bs, _ = y_blocks.shape
    size = rows * bs
    bf16, f32 = jnp.bfloat16, jnp.float32
    unit = (size, size)
    out = jax.ShapeDtypeStruct(y_blocks.shape, bf16)
    any_space = pl.BlockSpec(memory_space=pl.ANY)
    vmem = pl.BlockSpec(memory_space=pltpu.VMEM)
    return pl.pallas_call(
        functools.partial(step_kernel, (row_count, col_count, rows, bs)),
        out_shape=(out, out),
        in_specs=[any_space, any_space, any_space],
        out_specs=(vmem, vmem),
        scratch_shapes=[
            pltpu.VMEM((rows, lanes + 1, bs, bs), bf16),
            pltpu.VMEM((rows, lanes + 1, bs, bs), bf16),
            pltpu.VMEM(pattern.shape, jnp.int32),
            pltpu.VMEM((9, rows, size), jnp.int32),
            pltpu.VMEM((16, 128), jnp.int32),
            pltpu.SMEM((16, 128), jnp.int32),
            pltpu.VMEM((5,) + unit, bf16),
            pltpu.VMEM((5,) + unit, bf16),
            pltpu.VMEM((5,) + unit, bf16),
            pltpu.VMEM((5, 4) + unit, bf16),
            pltpu.VMEM(unit, bf16),
            pltpu.VMEM((4,) + unit, f32),
            pltpu.VMEM(unit, f32),
            pltpu.VMEM(unit, f32),
            pltpu.VMEM(unit, f32),
            pltpu.VMEM((5 * rows, rows, bs, bs), bf16),
            pltpu.VMEM((5 * rows, rows, bs, bs), bf16),
            pltpu.SemaphoreType.DMA((4,)),
            pltpu.SemaphoreType.DMA((5, 4)),
            pltpu.SemaphoreType.DMA((5, 4)),
        ],
        compiler_params=pltpu.CompilerParams(
            collective_id=0, has_side_effects=True, vmem_limit_bytes=56 << 20
        ),
    )(y_blocks, z_blocks, pattern)


def solution(mesh):
    spec = P(("row", "col"), None, None, None)
    return jax.shard_map(
        functools.partial(on_device, mesh.shape["row"], mesh.shape["col"]),
        mesh=mesh,
        in_specs=(spec, spec, P()),
        out_specs=(spec, spec),
        check_vma=False,
    )
```

```python
import functools

import jax
import jax.numpy as jnp
from jax import lax
from jax.experimental import pallas as pl
from jax.experimental.pallas import tpu as pltpu
from jax.sharding import PartitionSpec as P

MESH = pl.DeviceIdType.MESH
Y_EDGE, Y_DIAG, Z_EDGE, Z_DIAG, T_DIAG = range(5)
SEND_ORDER = (2, 3, 0, 1)


def step_kernel(
    layout,
    y_hbm, z_hbm, pat_hbm,
    y_out, z_out,
    y_raw, z_raw, pat, keep, tab_v, tab,
    y_own, z_own, t_own, got, t_near, y_part, acc, y_acc, z_acc,
    y_dense, z_dense,
    in_sem, send_sem, recv_sem,
):
    row_count, col_count, rows, bs = layout
    lanes = pat.shape[0]
    me_r, me_c = lax.axis_index("row"), lax.axis_index("col")

    def neighbour(d):
        if isinstance(d, int):
            step_r = (-1, 1, 0, 0)[d]
            step_c = (0, 0, -1, 1)[d]
        else:
            step_r = jnp.where(d < 2, 2 * d - 1, 0)
            step_c = jnp.where(d < 2, 0, 2 * d - 5)
        return (
            lax.rem(me_r + step_r + row_count, row_count),
            lax.rem(me_c + step_c + col_count, col_count),
        )

    barrier = pltpu.get_barrier_semaphore()
    for d in range(4):
        pl.semaphore_signal(barrier, 1, device_id=neighbour(d), device_id_type=MESH)
    copies = [
        pltpu.make_async_copy(pat_hbm, pat, in_sem.at[0]),
        pltpu.make_async_copy(y_hbm, y_raw.at[:, 0:lanes], in_sem.at[1]),
        pltpu.make_async_copy(z_hbm, z_raw.at[:, 0:lanes], in_sem.at[2]),
    ]
    for copy in copies:
        copy.start()

    for raw in (y_raw, z_raw):
        for i in range(rows):
            raw[i, lanes] = jnp.zeros((bs, bs), raw.dtype)

    at_near, at_back = 5 * rows, 9 * rows
    copies[0].wait()
    place = lax.broadcasted_iota(jnp.int32, (lanes, 128), 0)

    def base(where):
        return (where[0] * col_count + where[1]) * rows

    def pat_rows(start):
        whole = pat[:, pl.ds(pl.multiple_of(start // 128 * 128, 128), 128)]
        return pltpu.roll(whole, lax.rem(128 - lax.rem(start, 128), 128), 1)

    def find(columns, column):
        return jnp.min(jnp.where(columns == column, place, lanes), axis=0, keepdims=True)

    bases = [base((me_r, me_c))] + [base(neighbour(d)) for d in range(4)]
    own = pat_rows(bases[0])
    back = jnp.zeros((lanes, 128), jnp.int32)
    for u in range(5):
        for c in range(rows):
            q = u * rows + c
            tab_v[q : q + 1, :] = find(own, bases[u] + c)
            back = jnp.where(own == bases[u] + c, q, back)
    tab_v[at_back : at_back + lanes, :] = back
    for d in range(4):
        near = pat_rows(bases[1 + d])
        for c in range(rows):
            q = at_near + d * rows + c
            tab_v[q : q + 1, :] = find(near, bases[0] + c)
    to_scalar = pltpu.make_async_copy(tab_v, tab, in_sem.at[3])
    to_scalar.start()
    to_scalar.wait()

    def densify(raw, dense, u):
        def one(i, _):
            at_rows = pl.ds(pl.multiple_of(i * bs, bs), bs)
            for c in range(rows):
                dense[u, at_rows, c * bs : (c + 1) * bs] = raw[i, tab[u * rows + c, i]]
            return 0

        lax.fori_loop(0, rows, one, 0)

    def transfer(kind, d, source):
        back_d = d ^ 1 if isinstance(d, int) else d + 1 - 2 * lax.rem(d, 2)
        return pltpu.make_async_remote_copy(
            src_ref=source,
            dst_ref=got.at[kind, back_d],
            send_sem=send_sem.at[kind, d],
            recv_sem=recv_sem.at[kind, back_d],
            device_id=neighbour(d),
            device_id_type=MESH,
        )

    def arrival(kind, d):
        return pltpu.make_async_remote_copy(
            src_ref=got.at[kind, d],
            dst_ref=got.at[kind, d],
            send_sem=send_sem.at[kind, d],
            recv_sem=recv_sem.at[kind, d],
            device_id=neighbour(d),
            device_id_type=MESH,
        )

    sends = []

    def send(kind, d, source):
        copy = transfer(kind, d, source)
        copy.start()
        sends.append(copy)

    copies[1].wait()
    densify(y_raw, y_own, 3)
    pl.semaphore_wait(barrier, 4)
    send(Y_EDGE, 2, y_own.at[3])
    densify(y_raw, y_own, 4)
    send(Y_EDGE, 3, y_own.at[4])
    for d in (0, 1):
        densify(y_raw, y_own, 1 + d)
        send(Y_EDGE, d, y_own.at[1 + d])
    densify(y_raw, y_own, 0)
    for d in SEND_ORDER:
        send(Y_DIAG, d, y_own.at[0])
    copies[2].wait()
    for d in SEND_ORDER:
        densify(z_raw, z_own, 1 + d)
        send(Z_EDGE, d, z_own.at[1 + d])
    densify(z_raw, z_own, 0)
    for d in SEND_ORDER:
        send(Z_DIAG, d, z_own.at[0])

    for u in range(9):
        for c in range(rows):
            for i in range(rows):
                keep[u, i : i + 1, c * bs : (c + 1) * bs] = jnp.full(
                    (1, bs), tab[u * rows + c, i], jnp.int32
                )

    def dot(a, b):
        return jnp.dot(a, b, preferred_element_type=jnp.float32)

    def store_t(target, u, diagonal):
        def one(i, _):
            at_rows = pl.ds(pl.multiple_of(i * bs, bs), bs)
            value = -0.5 * acc[at_rows, :]
            if diagonal:
                r = lax.broadcasted_iota(jnp.int32, value.shape, 0) + i * bs
                s = lax.broadcasted_iota(jnp.int32, value.shape, 1)
                value = jnp.where(r == s, 1.5 + value, value)
            present = jnp.broadcast_to(keep[u, pl.ds(i, 1), :], value.shape) < lanes
            target[at_rows, :] = jnp.where(present, value, 0.0).astype(jnp.bfloat16)
            return 0

        lax.fori_loop(0, rows, one, 0)

    def store_blocks(blocks, u, source):
        def one(i, _):
            at_rows = pl.ds(pl.multiple_of(i * bs, bs), bs)
            for c in range(rows):
                block = source[at_rows, c * bs : (c + 1) * bs]
                blocks[u * rows + c, i] = block.astype(jnp.bfloat16)
            return 0

        lax.fori_loop(0, rows, one, 0)

    acc[...] = dot(z_own[0], y_own[0])

    def add_edge(d, _):
        arrival(Y_EDGE, d).wait_recv()
        acc[...] += dot(z_own[1 + d], got[Y_EDGE, d])
        return 0

    lax.fori_loop(0, 4, add_edge, 0)
    store_t(t_own.at[0], 0, True)
    for d in SEND_ORDER:
        send(T_DIAG, d, t_own.at[0])
    y_acc[...] = dot(y_own[0], t_own[0])
    z_acc[...] = dot(t_own[0], z_own[0])

    def t_edge(d, _):
        acc[...] = dot(z_own[0], y_own[1 + d])
        arrival(Y_DIAG, d).wait_recv()
        acc[...] += dot(z_own[1 + d], got[Y_DIAG, d])
        store_t(t_own.at[1 + d], 1 + d, False)
        y_part[d] = dot(y_own[0], t_own[1 + d])
        return 0

    lax.fori_loop(0, 4, t_edge, 0)

    def z_step(d, _):
        arrival(Z_EDGE, d).wait_recv()
        acc[...] = dot(got[Z_EDGE, d], y_own[0])
        z_acc[...] += dot(t_own[1 + d], got[Z_EDGE, d])
        arrival(Z_DIAG, d).wait_recv()
        acc[...] += dot(got[Z_DIAG, d], got[Y_EDGE, d])
        store_t(t_near, 5 + d, False)
        y_acc[...] += dot(y_own[1 + d], t_near[...])
        acc[...] = dot(t_own[0], z_own[1 + d])
        acc[...] += dot(t_own[1 + d], got[Z_DIAG, d])
        store_blocks(z_dense, 1 + d, acc)
        return 0

    lax.fori_loop(0, 4, z_step, 0)
    store_blocks(z_dense, 0, z_acc)
    store_blocks(y_dense, 0, y_acc)

    def gather(blocks, out):
        def one(i, _):
            for m in range(lanes):
                out[i, m] = blocks[tab[at_back + m, i], i]
            return 0

        lax.fori_loop(0, rows, one, 0)

    gather(z_dense, z_out)

    def y_step(d, _):
        arrival(T_DIAG, d).wait_recv()
        acc[...] = y_part[d] + dot(y_own[1 + d], got[T_DIAG, d])
        store_blocks(y_dense, 1 + d, acc)
        return 0

    lax.fori_loop(0, 4, y_step, 0)
    gather(y_dense, y_out)
    for copy in sends:
        copy.wait_send()


def write_kernel(y_vmem, z_vmem, y_out, z_out, sem):
    copies = []
    for n, (source, target) in enumerate(((z_vmem, z_out), (y_vmem, y_out))):
        for i in range(source.shape[0]):
            copies.append(pltpu.make_async_copy(source.at[i], target.at[i], sem.at[n, i]))
    for copy in copies:
        copy.start()
    for copy in copies:
        copy.wait()


def on_device(row_count, col_count, y_blocks, z_blocks, pattern):
    rows, lanes, bs, _ = y_blocks.shape
    size = rows * bs
    bf16, f32 = jnp.bfloat16, jnp.float32
    unit = (size, size)
    held = pltpu.VMEM(y_blocks.shape, bf16)
    out = jax.ShapeDtypeStruct(y_blocks.shape, bf16)
    any_space = pl.BlockSpec(memory_space=pl.ANY)
    vmem = pl.BlockSpec(memory_space=pltpu.VMEM)
    y_vmem, z_vmem = pl.pallas_call(
        functools.partial(step_kernel, (row_count, col_count, rows, bs)),
        out_shape=(held, held),
        in_specs=[any_space, any_space, any_space],
        out_specs=(vmem, vmem),
        scratch_shapes=[
            pltpu.VMEM((rows, lanes + 1, bs, bs), bf16),
            pltpu.VMEM((rows, lanes + 1, bs, bs), bf16),
            pltpu.VMEM((lanes, pattern.shape[0]), jnp.int32),
            pltpu.VMEM((9, rows, size), jnp.int32),
            pltpu.VMEM((9 * rows + lanes, 128), jnp.int32),
            pltpu.SMEM((9 * rows + lanes, 128), jnp.int32),
            pltpu.VMEM((5,) + unit, bf16),
            pltpu.VMEM((5,) + unit, bf16),
            pltpu.VMEM((5,) + unit, bf16),
            pltpu.VMEM((5, 4) + unit, bf16),
            pltpu.VMEM(unit, bf16),
            pltpu.VMEM((4,) + unit, f32),
            pltpu.VMEM(unit, f32),
            pltpu.VMEM(unit, f32),
            pltpu.VMEM(unit, f32),
            pltpu.VMEM((5 * rows, rows, bs, bs), bf16),
            pltpu.VMEM((5 * rows, rows, bs, bs), bf16),
            pltpu.SemaphoreType.DMA((4,)),
            pltpu.SemaphoreType.DMA((5, 4)),
            pltpu.SemaphoreType.DMA((5, 4)),
        ],
        compiler_params=pltpu.CompilerParams(
            collective_id=0, has_side_effects=True, vmem_limit_bytes=48 << 20
        ),
    )(y_blocks, z_blocks, pltpu.with_memory_space_constraint(pattern.T, pltpu.HBM))
    return pl.pallas_call(
        write_kernel,
        out_shape=(out, out),
        in_specs=[vmem, vmem],
        out_specs=(any_space, any_space),
        scratch_shapes=[pltpu.SemaphoreType.DMA((2, rows))],
        compiler_params=pltpu.CompilerParams(vmem_limit_bytes=1 << 20),
    )(
        pltpu.with_memory_space_constraint(y_vmem, pltpu.VMEM),
        pltpu.with_memory_space_constraint(z_vmem, pltpu.VMEM),
    )


def solution(mesh):
    spec = P(("row", "col"), None, None, None)
    return jax.shard_map(
        functools.partial(on_device, mesh.shape["row"], mesh.shape["col"]),
        mesh=mesh,
        in_specs=(spec, spec, P()),
        out_specs=(spec, spec),
        check_vma=False,
    )
```

```python
import functools

import jax
import jax.numpy as jnp
from jax import lax
from jax.experimental import pallas as pl
from jax.experimental.pallas import tpu as pltpu
from jax.sharding import PartitionSpec as P

MESH = pl.DeviceIdType.MESH
Y_EDGE, Y_DIAG, Z_EDGE, Z_DIAG, T_DIAG = range(5)
T_PARTS = 2
SEND_ORDER = (2, 3, 0, 1)


def step_kernel(
    layout,
    y_hbm, z_hbm, pat_hbm,
    y_out, z_out,
    y_raw, z_raw, pat, keep, tab_v, tab,
    y_own, z_own, t_own, got, t_near, y_part, acc, y_acc, z_acc,
    y_dense, z_dense,
    in_sem, send_sem, recv_sem,
):
    row_count, col_count, rows, bs = layout
    lanes = pat.shape[0]
    me_r, me_c = lax.axis_index("row"), lax.axis_index("col")

    def neighbour(d):
        if isinstance(d, int):
            step_r = (-1, 1, 0, 0)[d]
            step_c = (0, 0, -1, 1)[d]
        else:
            step_r = jnp.where(d < 2, 2 * d - 1, 0)
            step_c = jnp.where(d < 2, 0, 2 * d - 5)
        return (
            lax.rem(me_r + step_r + row_count, row_count),
            lax.rem(me_c + step_c + col_count, col_count),
        )

    barrier = pltpu.get_barrier_semaphore()
    for d in range(4):
        pl.semaphore_signal(barrier, 1, device_id=neighbour(d), device_id_type=MESH)
    copies = [
        pltpu.make_async_copy(pat_hbm, pat, in_sem.at[0]),
        pltpu.make_async_copy(y_hbm, y_raw.at[:, 0:lanes], in_sem.at[1]),
        pltpu.make_async_copy(z_hbm, z_raw.at[:, 0:lanes], in_sem.at[2]),
    ]
    for copy in copies:
        copy.start()

    for raw in (y_raw, z_raw):
        for i in range(rows):
            raw[i, lanes] = jnp.zeros((bs, bs), raw.dtype)

    at_near, at_back = 5 * rows, 9 * rows
    copies[0].wait()
    place = lax.broadcasted_iota(jnp.int32, (lanes, 128), 0)

    def base(where):
        return (where[0] * col_count + where[1]) * rows

    def pat_rows(start):
        whole = pat[:, pl.ds(pl.multiple_of(start // 128 * 128, 128), 128)]
        return pltpu.roll(whole, lax.rem(128 - lax.rem(start, 128), 128), 1)

    def find(columns, column):
        return jnp.min(jnp.where(columns == column, place, lanes), axis=0, keepdims=True)

    bases = [base((me_r, me_c))] + [base(neighbour(d)) for d in range(4)]
    own = pat_rows(bases[0])
    back = jnp.zeros((lanes, 128), jnp.int32)
    for u in range(5):
        for c in range(rows):
            q = u * rows + c
            tab_v[q : q + 1, :] = find(own, bases[u] + c)
            back = jnp.where(own == bases[u] + c, q, back)
    tab_v[at_back : at_back + lanes, :] = back
    for d in range(4):
        near = pat_rows(bases[1 + d])
        for c in range(rows):
            q = at_near + d * rows + c
            tab_v[q : q + 1, :] = find(near, bases[0] + c)
    to_scalar = pltpu.make_async_copy(tab_v, tab, in_sem.at[3])
    to_scalar.start()
    to_scalar.wait()

    def densify(raw, dense, u):
        def one(i, _):
            at_rows = pl.ds(pl.multiple_of(i * bs, bs), bs)
            for c in range(rows):
                dense[u, at_rows, c * bs : (c + 1) * bs] = raw[i, tab[u * rows + c, i]]
            return 0

        lax.fori_loop(0, rows, one, 0)

    size = rows * bs
    width = size // T_PARTS

    def target(kind, d):
        if kind < T_DIAG:
            return got.at[kind, d]
        n = kind - T_DIAG
        return got.at[T_DIAG, d, :, n * width : (n + 1) * width]

    def transfer(kind, d, source):
        return pltpu.make_async_remote_copy(
            src_ref=source,
            dst_ref=target(kind, d ^ 1),
            send_sem=send_sem.at[kind, d],
            recv_sem=recv_sem.at[kind, d ^ 1],
            device_id=neighbour(d),
            device_id_type=MESH,
        )

    def arrival(kind, d):
        return pltpu.make_async_remote_copy(
            src_ref=target(kind, d),
            dst_ref=target(kind, d),
            send_sem=send_sem.at[kind, d],
            recv_sem=recv_sem.at[kind, d],
            device_id=neighbour(d),
            device_id_type=MESH,
        )

    sends = []

    def send(kind, d, source):
        copy = transfer(kind, d, source)
        copy.start()
        sends.append(copy)

    copies[1].wait()
    densify(y_raw, y_own, 3)
    pl.semaphore_wait(barrier, 4)
    send(Y_EDGE, 2, y_own.at[3])
    densify(y_raw, y_own, 4)
    send(Y_EDGE, 3, y_own.at[4])
    for d in (0, 1):
        densify(y_raw, y_own, 1 + d)
        send(Y_EDGE, d, y_own.at[1 + d])
    densify(y_raw, y_own, 0)
    for d in SEND_ORDER:
        send(Y_DIAG, d, y_own.at[0])
    copies[2].wait()
    for d in SEND_ORDER:
        densify(z_raw, z_own, 1 + d)
        send(Z_EDGE, d, z_own.at[1 + d])
    densify(z_raw, z_own, 0)
    for d in SEND_ORDER:
        send(Z_DIAG, d, z_own.at[0])

    for u in range(9):
        for c in range(rows):
            for i in range(rows):
                keep[u, i : i + 1, c * bs : (c + 1) * bs] = jnp.full(
                    (1, bs), tab[u * rows + c, i], jnp.int32
                )

    def dot(a, b):
        return jnp.dot(a, b, preferred_element_type=jnp.float32)

    def store_t(target, u, diagonal):
        def one(i, _):
            at_rows = pl.ds(pl.multiple_of(i * bs, bs), bs)
            value = -0.5 * acc[at_rows, :]
            if diagonal:
                r = lax.broadcasted_iota(jnp.int32, value.shape, 0) + i * bs
                s = lax.broadcasted_iota(jnp.int32, value.shape, 1)
                value = jnp.where(r == s, 1.5 + value, value)
            present = jnp.broadcast_to(keep[u, pl.ds(i, 1), :], value.shape) < lanes
            target[at_rows, :] = jnp.where(present, value, 0.0).astype(jnp.bfloat16)
            return 0

        lax.fori_loop(0, rows, one, 0)

    def store_blocks(blocks, u, source):
        def one(i, _):
            at_rows = pl.ds(pl.multiple_of(i * bs, bs), bs)
            for c in range(rows):
                block = source[at_rows, c * bs : (c + 1) * bs]
                blocks[u * rows + c, i] = block.astype(jnp.bfloat16)
            return 0

        lax.fori_loop(0, rows, one, 0)

    acc[...] = dot(z_own[0], y_own[0])

    def add_edge(d, _):
        arrival(Y_EDGE, d).wait_recv()
        acc[...] += dot(z_own[1 + d], got[Y_EDGE, d])
        return 0

    lax.fori_loop(0, 4, add_edge, 0)
    store_t(t_own.at[0], 0, True)
    for n in range(T_PARTS):
        for d in SEND_ORDER:
            send(T_DIAG + n, d, t_own.at[0, :, n * width : (n + 1) * width])
    y_acc[...] = dot(y_own[0], t_own[0])
    z_acc[...] = dot(t_own[0], z_own[0])

    def t_edge(d, _):
        acc[...] = dot(z_own[0], y_own[1 + d])
        arrival(Y_DIAG, d).wait_recv()
        acc[...] += dot(z_own[1 + d], got[Y_DIAG, d])
        store_t(t_own.at[1 + d], 1 + d, False)
        y_part[d] = dot(y_own[0], t_own[1 + d])
        return 0

    lax.fori_loop(0, 4, t_edge, 0)

    def z_step(d, _):
        arrival(Z_EDGE, d).wait_recv()
        acc[...] = dot(got[Z_EDGE, d], y_own[0])
        z_acc[...] += dot(t_own[1 + d], got[Z_EDGE, d])
        arrival(Z_DIAG, d).wait_recv()
        acc[...] += dot(got[Z_DIAG, d], got[Y_EDGE, d])
        store_t(t_near, 5 + d, False)
        y_acc[...] += dot(y_own[1 + d], t_near[...])
        acc[...] = dot(t_own[0], z_own[1 + d])
        acc[...] += dot(t_own[1 + d], got[Z_DIAG, d])
        store_blocks(z_dense, 1 + d, acc)
        return 0

    lax.fori_loop(0, 4, z_step, 0)
    store_blocks(z_dense, 0, z_acc)
    store_blocks(y_dense, 0, y_acc)

    def gather(blocks, out):
        def one(i, _):
            for m in range(lanes):
                out[i, m] = blocks[tab[at_back + m, i], i]
            return 0

        lax.fori_loop(0, rows, one, 0)

    gather(z_dense, z_out)

    for n in range(T_PARTS):
        cols = slice(n * width, (n + 1) * width)

        def y_step(d, _):
            arrival(T_DIAG + n, d).wait_recv()
            part = dot(y_own[1 + d], got[T_DIAG, d, :, cols]) + y_part[d, :, cols]
            part = part.astype(jnp.bfloat16)
            for i in range(rows):
                for c in range(width // bs):
                    q = (1 + d) * rows + n * (width // bs) + c
                    y_dense[q, i] = part[i * bs : (i + 1) * bs, c * bs : (c + 1) * bs]
            return 0

        lax.fori_loop(0, 4, y_step, 0)
    gather(y_dense, y_out)
    for copy in sends:
        copy.wait_send()


def write_kernel(y_vmem, z_vmem, y_out, z_out, sem):
    copies = []
    for n, (source, target) in enumerate(((z_vmem, z_out), (y_vmem, y_out))):
        copies.append(pltpu.make_async_copy(source, target, sem.at[n, 0]))
    for copy in copies:
        copy.start()
    for copy in copies:
        copy.wait()


def on_device(row_count, col_count, y_blocks, z_blocks, pattern):
    rows, lanes, bs, _ = y_blocks.shape
    size = rows * bs
    bf16, f32 = jnp.bfloat16, jnp.float32
    unit = (size, size)
    held = pltpu.VMEM(y_blocks.shape, bf16)
    out = jax.ShapeDtypeStruct(y_blocks.shape, bf16)
    any_space = pl.BlockSpec(memory_space=pl.ANY)
    vmem = pl.BlockSpec(memory_space=pltpu.VMEM)
    y_vmem, z_vmem = pl.pallas_call(
        functools.partial(step_kernel, (row_count, col_count, rows, bs)),
        out_shape=(held, held),
        in_specs=[any_space, any_space, any_space],
        out_specs=(vmem, vmem),
        scratch_shapes=[
            pltpu.VMEM((rows, lanes + 1, bs, bs), bf16),
            pltpu.VMEM((rows, lanes + 1, bs, bs), bf16),
            pltpu.VMEM((lanes, pattern.shape[0]), jnp.int32),
            pltpu.VMEM((9, rows, size), jnp.int32),
            pltpu.VMEM((9 * rows + lanes, 128), jnp.int32),
            pltpu.SMEM((9 * rows + lanes, 128), jnp.int32),
            pltpu.VMEM((5,) + unit, bf16),
            pltpu.VMEM((5,) + unit, bf16),
            pltpu.VMEM((5,) + unit, bf16),
            pltpu.VMEM((5, 4) + unit, bf16),
            pltpu.VMEM(unit, bf16),
            pltpu.VMEM((4,) + unit, f32),
            pltpu.VMEM(unit, f32),
            pltpu.VMEM(unit, f32),
            pltpu.VMEM(unit, f32),
            pltpu.VMEM((5 * rows, rows, bs, bs), bf16),
            pltpu.VMEM((5 * rows, rows, bs, bs), bf16),
            pltpu.SemaphoreType.DMA((4,)),
            pltpu.SemaphoreType.DMA((4 + T_PARTS, 4)),
            pltpu.SemaphoreType.DMA((4 + T_PARTS, 4)),
        ],
        compiler_params=pltpu.CompilerParams(
            collective_id=0, has_side_effects=True, vmem_limit_bytes=48 << 20
        ),
    )(y_blocks, z_blocks, pltpu.with_memory_space_constraint(pattern.T, pltpu.HBM))
    return pl.pallas_call(
        write_kernel,
        out_shape=(out, out),
        in_specs=[vmem, vmem],
        out_specs=(any_space, any_space),
        scratch_shapes=[pltpu.SemaphoreType.DMA((2, rows))],
        compiler_params=pltpu.CompilerParams(vmem_limit_bytes=1 << 20),
    )(
        pltpu.with_memory_space_constraint(y_vmem, pltpu.VMEM),
        pltpu.with_memory_space_constraint(z_vmem, pltpu.VMEM),
    )


def solution(mesh):
    spec = P(("row", "col"), None, None, None)
    return jax.shard_map(
        functools.partial(on_device, mesh.shape["row"], mesh.shape["col"]),
        mesh=mesh,
        in_specs=(spec, spec, P()),
        out_specs=(spec, spec),
        check_vma=False,
    )
```

```python
import functools

import jax
import jax.numpy as jnp
from jax import lax
from jax.experimental import pallas as pl
from jax.experimental.pallas import tpu as pltpu
from jax.sharding import PartitionSpec as P

MESH = pl.DeviceIdType.MESH
Y_EDGE, Y_DIAG, Z_EDGE, Z_DIAG, T_DIAG = range(5)
T_PARTS = (2, 1, 1)
T_KINDS = len(T_PARTS) + 1
LAP = 4
SEND_ORDER = (2, 3, 0, 1)


def step_kernel(
    layout,
    y_hbm, z_hbm, pat_hbm,
    y_out, z_out,
    y_raw, z_raw, pat, keep, tab_v, tab,
    y_own, z_own, t_own, got, t_near, y_part, acc, y_acc, z_acc,
    y_dense, z_dense,
    relay_buf, in_sem, send_sem, recv_sem, relay_sem, entered,
):
    row_count, col_count, rows, bs = layout
    lanes = pat.shape[0]
    me_r, me_c = lax.axis_index("row"), lax.axis_index("col")

    def neighbour(d):
        if isinstance(d, int):
            step_r = (-1, 1, 0, 0)[d]
            step_c = (0, 0, -1, 1)[d]
        else:
            step_r = jnp.where(d < 2, 2 * d - 1, 0)
            step_c = jnp.where(d < 2, 0, 2 * d - 5)
        return (
            lax.rem(me_r + step_r + row_count, row_count),
            lax.rem(me_c + step_c + col_count, col_count),
        )

    barrier = pltpu.get_barrier_semaphore()
    detours = (me_c == LAP - 1, me_c == col_count - 1)
    detours = (detours[1], detours[0] | detours[1])
    relays = (me_c == LAP - 1, (me_c == LAP - 1) | (me_c == 2 * LAP - 1))
    ends = (me_c == 0) | (me_c == LAP)
    relay_place = (me_r, lax.rem(me_c + LAP, col_count))
    end_place = (me_r, lax.rem(me_c + col_count + 1 - LAP, col_count))

    def greet(place):
        pl.semaphore_signal(barrier, 1, device_id=place, device_id_type=MESH)

    for d in (0, 1, 2):
        greet(neighbour(d))
    pl.when(relays[1])(lambda: greet((me_r, lax.rem(me_c + col_count - LAP, col_count))))
    pl.when(ends)(lambda: greet((me_r, lax.rem(me_c + LAP - 1, col_count))))
    copies = [
        pltpu.make_async_copy(pat_hbm, pat, in_sem.at[0]),
        pltpu.make_async_copy(y_hbm, y_raw.at[:, 0:lanes], in_sem.at[1]),
        pltpu.make_async_copy(z_hbm, z_raw.at[:, 0:lanes], in_sem.at[2]),
    ]
    for copy in copies:
        copy.start()

    for raw in (y_raw, z_raw):
        for i in range(rows):
            raw[i, lanes] = jnp.zeros((bs, bs), raw.dtype)

    at_near, at_back = 5 * rows, 9 * rows
    copies[0].wait()
    place = lax.broadcasted_iota(jnp.int32, (lanes, 128), 0)

    def base(where):
        return (where[0] * col_count + where[1]) * rows

    def pat_rows(start):
        whole = pat[:, pl.ds(pl.multiple_of(start // 128 * 128, 128), 128)]
        return pltpu.roll(whole, lax.rem(128 - lax.rem(start, 128), 128), 1)

    def find(columns, column):
        return jnp.min(jnp.where(columns == column, place, lanes), axis=0, keepdims=True)

    bases = [base((me_r, me_c))] + [base(neighbour(d)) for d in range(4)]
    own = pat_rows(bases[0])
    back = jnp.zeros((lanes, 128), jnp.int32)
    for u in range(5):
        for c in range(rows):
            q = u * rows + c
            tab_v[q : q + 1, :] = find(own, bases[u] + c)
            back = jnp.where(own == bases[u] + c, q, back)
    tab_v[at_back : at_back + lanes, :] = back
    for d in range(4):
        near = pat_rows(bases[1 + d])
        for c in range(rows):
            q = at_near + d * rows + c
            tab_v[q : q + 1, :] = find(near, bases[0] + c)
    to_scalar = pltpu.make_async_copy(tab_v, tab, in_sem.at[3])
    to_scalar.start()
    pl.semaphore_wait(barrier, 3 + jnp.where(detours[1], 1, 0) + jnp.where(relays[1], 1, 0))
    pl.semaphore_signal(entered, 1, device_id=neighbour(3), device_id_type=MESH)
    to_scalar.wait()

    def densify(raw, dense, u):
        def one(i, _):
            at_rows = pl.ds(pl.multiple_of(i * bs, bs), bs)
            for c in range(rows):
                dense[u, at_rows, c * bs : (c + 1) * bs] = raw[i, tab[u * rows + c, i]]
            return 0

        lax.fori_loop(0, rows, one, 0)

    size = rows * bs
    part_cols = []
    for n, width in enumerate(T_PARTS):
        start = sum(T_PARTS[:n]) * bs
        part_cols.append(slice(start, start + width * bs))
    pieces = [(slice(0, size), cols) for cols in part_cols[:-1]]
    pieces += [(slice(0, size // 2), part_cols[-1]), (slice(size // 2, size), part_cols[-1])]

    def target(kind, d):
        if kind < T_DIAG:
            return got.at[kind, d]
        at_rows, cols = pieces[kind - T_DIAG]
        return got.at[T_DIAG, d, at_rows, cols]

    def transfer(kind, d, source):
        return pltpu.make_async_remote_copy(
            src_ref=source,
            dst_ref=target(kind, d ^ 1),
            send_sem=send_sem.at[kind, d],
            recv_sem=recv_sem.at[kind, d ^ 1],
            device_id=neighbour(d),
            device_id_type=MESH,
        )

    def arrival(kind, d):
        return pltpu.make_async_remote_copy(
            src_ref=target(kind, d),
            dst_ref=target(kind, d),
            send_sem=send_sem.at[kind, d],
            recv_sem=recv_sem.at[kind, d],
            device_id=neighbour(d),
            device_id_type=MESH,
        )

    sends = []

    def send(kind, d, source):
        copy = transfer(kind, d, source)
        copy.start()
        sends.append(copy)

    copies[1].wait()
    densify(y_raw, y_own, 4)
    send(Y_EDGE, 3, y_own.at[4])
    for d in (0, 1):
        densify(y_raw, y_own, 1 + d)
        send(Y_EDGE, d, y_own.at[1 + d])
    densify(y_raw, y_own, 0)
    densify(y_raw, y_own, 3)
    for d in (3, 0, 1):
        send(Y_DIAG, d, y_own.at[0])
    pl.semaphore_wait(entered, 1)
    send(Y_EDGE, 2, y_own.at[3])
    send(Y_DIAG, 2, y_own.at[0])
    copies[2].wait()
    for d in SEND_ORDER:
        densify(z_raw, z_own, 1 + d)
        send(Z_EDGE, d, z_own.at[1 + d])
    densify(z_raw, z_own, 0)
    for d in SEND_ORDER:
        send(Z_DIAG, d, z_own.at[0])

    for u in range(9):
        for c in range(rows):
            for i in range(rows):
                keep[u, i : i + 1, c * bs : (c + 1) * bs] = jnp.full(
                    (1, bs), tab[u * rows + c, i], jnp.int32
                )

    def dot(a, b):
        return jnp.dot(a, b, preferred_element_type=jnp.float32)

    def store_t(target, u, diagonal):
        def one(i, _):
            at_rows = pl.ds(pl.multiple_of(i * bs, bs), bs)
            value = -0.5 * acc[at_rows, :]
            if diagonal:
                r = lax.broadcasted_iota(jnp.int32, value.shape, 0) + i * bs
                s = lax.broadcasted_iota(jnp.int32, value.shape, 1)
                value = jnp.where(r == s, 1.5 + value, value)
            present = jnp.broadcast_to(keep[u, pl.ds(i, 1), :], value.shape) < lanes
            target[at_rows, :] = jnp.where(present, value, 0.0).astype(jnp.bfloat16)
            return 0

        lax.fori_loop(0, rows, one, 0)

    def store_blocks(blocks, u, source):
        def one(i, _):
            at_rows = pl.ds(pl.multiple_of(i * bs, bs), bs)
            for c in range(rows):
                block = source[at_rows, c * bs : (c + 1) * bs]
                blocks[u * rows + c, i] = block.astype(jnp.bfloat16)
            return 0

        lax.fori_loop(0, rows, one, 0)

    acc[...] = dot(z_own[0], y_own[0])

    def add_edge(d, _):
        arrival(Y_EDGE, d).wait_recv()
        acc[...] += dot(z_own[1 + d], got[Y_EDGE, d])
        return 0

    lax.fori_loop(0, 4, add_edge, 0)
    store_t(t_own.at[0], 0, True)
    hops, forwards = [], []
    for p in range(2):
        kind = T_DIAG + T_KINDS - 2 + p
        hops.append(
            pltpu.make_async_remote_copy(
                src_ref=t_own.at[0, pieces[kind - T_DIAG][0], pieces[kind - T_DIAG][1]],
                dst_ref=relay_buf.at[p],
                send_sem=send_sem.at[kind, 3],
                recv_sem=relay_sem.at[p, 0],
                device_id=relay_place,
                device_id_type=MESH,
            )
        )
        forwards.append(
            pltpu.make_async_remote_copy(
                src_ref=relay_buf.at[p],
                dst_ref=target(kind, 2),
                send_sem=relay_sem.at[p, 1],
                recv_sem=recv_sem.at[kind, 2],
                device_id=end_place,
                device_id_type=MESH,
            )
        )
    for n in range(T_KINDS):
        p = n - (T_KINDS - 2)
        for d in SEND_ORDER:
            source = t_own.at[0, pieces[n][0], pieces[n][1]]
            if p >= 0 and d == 3:
                direct = transfer(T_DIAG + n, d, source)
                pl.when(detours[p])(hops[p].start)
                pl.when(jnp.logical_not(detours[p]))(direct.start)
                sends.append(direct)
            else:
                send(T_DIAG + n, d, source)
    y_acc[...] = dot(y_own[0], t_own[0])
    z_acc[...] = dot(t_own[0], z_own[0])

    def t_edge(d, _):
        acc[...] = dot(z_own[0], y_own[1 + d])
        arrival(Y_DIAG, d).wait_recv()
        acc[...] += dot(z_own[1 + d], got[Y_DIAG, d])
        store_t(t_own.at[1 + d], 1 + d, False)
        y_part[d] = dot(y_own[0], t_own[1 + d])
        return 0

    lax.fori_loop(0, 4, t_edge, 0)

    def pass_on(p):
        hops[p].wait_recv()
        forwards[p].start()

    for p in range(2):
        pl.when(relays[p])(functools.partial(pass_on, p))

    def z_step(d, _):
        arrival(Z_EDGE, d).wait_recv()
        acc[...] = dot(got[Z_EDGE, d], y_own[0])
        z_acc[...] += dot(t_own[1 + d], got[Z_EDGE, d])
        arrival(Z_DIAG, d).wait_recv()
        acc[...] += dot(got[Z_DIAG, d], got[Y_EDGE, d])
        store_t(t_near, 5 + d, False)
        y_acc[...] += dot(y_own[1 + d], t_near[...])
        acc[...] = dot(t_own[0], z_own[1 + d])
        acc[...] += dot(t_own[1 + d], got[Z_DIAG, d])
        store_blocks(z_dense, 1 + d, acc)
        return 0

    lax.fori_loop(0, 4, z_step, 0)
    store_blocks(z_dense, 0, z_acc)
    store_blocks(y_dense, 0, y_acc)

    def gather(blocks, out):
        def one(i, _):
            for m in range(lanes):
                out[i, m] = blocks[tab[at_back + m, i], i]
            return 0

        lax.fori_loop(0, rows, one, 0)

    gather(z_dense, z_out)

    for n, width in enumerate(T_PARTS):
        cols = part_cols[n]

        def y_step(d, _):
            arrival(T_DIAG + n, d).wait_recv()
            if n == len(T_PARTS) - 1:
                arrival(T_DIAG + n + 1, d).wait_recv()
            part = dot(y_own[1 + d], got[T_DIAG, d, :, cols]) + y_part[d, :, cols]
            part = part.astype(jnp.bfloat16)
            for i in range(rows):
                for c in range(width):
                    q = (1 + d) * rows + sum(T_PARTS[:n]) + c
                    y_dense[q, i] = part[i * bs : (i + 1) * bs, c * bs : (c + 1) * bs]
            return 0

        lax.fori_loop(0, 4, y_step, 0)
    gather(y_dense, y_out)
    for copy in sends:
        copy.wait_send()
    for p in range(2):
        pl.when(relays[p])(forwards[p].wait_send)


def write_kernel(y_vmem, z_vmem, y_out, z_out, sem):
    copies = []
    for n, (source, target) in enumerate(((z_vmem, z_out), (y_vmem, y_out))):
        copies.append(pltpu.make_async_copy(source, target, sem.at[n, 0]))
    for copy in copies:
        copy.start()
    for copy in copies:
        copy.wait()


def on_device(row_count, col_count, y_blocks, z_blocks, pattern):
    rows, lanes, bs, _ = y_blocks.shape
    size = rows * bs
    bf16, f32 = jnp.bfloat16, jnp.float32
    unit = (size, size)
    held = pltpu.VMEM(y_blocks.shape, bf16)
    out = jax.ShapeDtypeStruct(y_blocks.shape, bf16)
    any_space = pl.BlockSpec(memory_space=pl.ANY)
    vmem = pl.BlockSpec(memory_space=pltpu.VMEM)
    y_vmem, z_vmem = pl.pallas_call(
        functools.partial(step_kernel, (row_count, col_count, rows, bs)),
        out_shape=(held, held),
        in_specs=[any_space, any_space, any_space],
        out_specs=(vmem, vmem),
        scratch_shapes=[
            pltpu.VMEM((rows, lanes + 1, bs, bs), bf16),
            pltpu.VMEM((rows, lanes + 1, bs, bs), bf16),
            pltpu.VMEM((lanes, pattern.shape[0]), jnp.int32),
            pltpu.VMEM((9, rows, size), jnp.int32),
            pltpu.VMEM((9 * rows + lanes, 128), jnp.int32),
            pltpu.SMEM((9 * rows + lanes, 128), jnp.int32),
            pltpu.VMEM((5,) + unit, bf16),
            pltpu.VMEM((5,) + unit, bf16),
            pltpu.VMEM((5,) + unit, bf16),
            pltpu.VMEM((5, 4) + unit, bf16),
            pltpu.VMEM(unit, bf16),
            pltpu.VMEM((4,) + unit, f32),
            pltpu.VMEM(unit, f32),
            pltpu.VMEM(unit, f32),
            pltpu.VMEM(unit, f32),
            pltpu.VMEM((5 * rows, rows, bs, bs), bf16),
            pltpu.VMEM((5 * rows, rows, bs, bs), bf16),
            pltpu.VMEM((2, size // 2, T_PARTS[-1] * bs), bf16),
            pltpu.SemaphoreType.DMA((4,)),
            pltpu.SemaphoreType.DMA((4 + T_KINDS, 4)),
            pltpu.SemaphoreType.DMA((4 + T_KINDS, 4)),
            pltpu.SemaphoreType.DMA((2, 2)),
            pltpu.SemaphoreType.REGULAR,
        ],
        compiler_params=pltpu.CompilerParams(
            collective_id=0, has_side_effects=True, vmem_limit_bytes=48 << 20
        ),
    )(y_blocks, z_blocks, pltpu.with_memory_space_constraint(pattern.T, pltpu.HBM))
    return pl.pallas_call(
        write_kernel,
        out_shape=(out, out),
        in_specs=[vmem, vmem],
        out_specs=(any_space, any_space),
        scratch_shapes=[pltpu.SemaphoreType.DMA((2, rows))],
        compiler_params=pltpu.CompilerParams(vmem_limit_bytes=1 << 20),
    )(
        pltpu.with_memory_space_constraint(y_vmem, pltpu.VMEM),
        pltpu.with_memory_space_constraint(z_vmem, pltpu.VMEM),
    )


def solution(mesh):
    spec = P(("row", "col"), None, None, None)
    return jax.shard_map(
        functools.partial(on_device, mesh.shape["row"], mesh.shape["col"]),
        mesh=mesh,
        in_specs=(spec, spec, P()),
        out_specs=(spec, spec),
        check_vma=False,
    )
```

```python
import functools

import jax
import jax.numpy as jnp
from jax import lax
from jax.experimental import pallas as pl
from jax.experimental.pallas import tpu as pltpu
from jax.sharding import PartitionSpec as P

MESH = pl.DeviceIdType.MESH
Y_EDGE, Y_DIAG, Z_EDGE, Z_DIAG, T_DIAG = range(5)
T_PARTS = (2, 1, 1)
T_KINDS = len(T_PARTS) + 1
LAP = 4
SEND_ORDER = (3, 2, 0, 1)


def step_kernel(
    layout,
    y_hbm, z_hbm, pat_hbm,
    y_out, z_out,
    y_raw, z_raw, pat, keep, tab_v, tab,
    y_own, z_own, t_own, got, t_near, y_part, acc, y_acc, z_acc,
    y_dense, z_dense,
    relay_buf, in_sem, send_sem, recv_sem, relay_sem, entered,
):
    row_count, col_count, rows, bs = layout
    lanes = pat.shape[0]
    me_r, me_c = lax.axis_index("row"), lax.axis_index("col")

    def neighbour(d):
        if isinstance(d, int):
            step_r = (-1, 1, 0, 0)[d]
            step_c = (0, 0, -1, 1)[d]
        else:
            step_r = jnp.where(d < 2, 2 * d - 1, 0)
            step_c = jnp.where(d < 2, 0, 2 * d - 5)
        return (
            lax.rem(me_r + step_r + row_count, row_count),
            lax.rem(me_c + step_c + col_count, col_count),
        )

    barrier = pltpu.get_barrier_semaphore()
    detours = (me_c == LAP - 1, me_c == col_count - 1)
    detours = (detours[1], detours[0] | detours[1])
    relays = (me_c == LAP - 1, (me_c == LAP - 1) | (me_c == 2 * LAP - 1))
    ends = (me_c == 0) | (me_c == LAP)
    relay_place = (me_r, lax.rem(me_c + LAP, col_count))
    end_place = (me_r, lax.rem(me_c + col_count + 1 - LAP, col_count))

    def greet(place):
        pl.semaphore_signal(barrier, 1, device_id=place, device_id_type=MESH)

    for d in (0, 1, 2):
        greet(neighbour(d))
    pl.when(relays[1])(lambda: greet((me_r, lax.rem(me_c + col_count - LAP, col_count))))
    pl.when(ends)(lambda: greet((me_r, lax.rem(me_c + LAP - 1, col_count))))
    copies = [
        pltpu.make_async_copy(pat_hbm, pat, in_sem.at[0]),
        pltpu.make_async_copy(y_hbm, y_raw.at[:, 0:lanes], in_sem.at[1]),
        pltpu.make_async_copy(z_hbm, z_raw.at[:, 0:lanes], in_sem.at[2]),
    ]
    for copy in copies:
        copy.start()

    for raw in (y_raw, z_raw):
        for i in range(rows):
            raw[i, lanes] = jnp.zeros((bs, bs), raw.dtype)

    at_near, at_back = 5 * rows, 9 * rows
    copies[0].wait()
    place = lax.broadcasted_iota(jnp.int32, (lanes, 128), 0)

    def base(where):
        return (where[0] * col_count + where[1]) * rows

    def pat_rows(start):
        whole = pat[:, pl.ds(pl.multiple_of(start // 128 * 128, 128), 128)]
        return pltpu.roll(whole, lax.rem(128 - lax.rem(start, 128), 128), 1)

    def find(columns, column):
        return jnp.min(jnp.where(columns == column, place, lanes), axis=0, keepdims=True)

    bases = [base((me_r, me_c))] + [base(neighbour(d)) for d in range(4)]
    own = pat_rows(bases[0])
    back = jnp.zeros((lanes, 128), jnp.int32)
    for u in range(5):
        for c in range(rows):
            q = u * rows + c
            tab_v[q : q + 1, :] = find(own, bases[u] + c)
            back = jnp.where(own == bases[u] + c, q, back)
    tab_v[at_back : at_back + lanes, :] = back
    for d in range(4):
        near = pat_rows(bases[1 + d])
        for c in range(rows):
            q = at_near + d * rows + c
            tab_v[q : q + 1, :] = find(near, bases[0] + c)
    to_scalar = pltpu.make_async_copy(tab_v, tab, in_sem.at[3])
    to_scalar.start()
    pl.semaphore_wait(barrier, 3 + jnp.where(detours[1], 1, 0) + jnp.where(relays[1], 1, 0))
    pl.semaphore_signal(entered, 1, device_id=neighbour(3), device_id_type=MESH)
    to_scalar.wait()

    def densify(raw, dense, u):
        def one(i, _):
            at_rows = pl.ds(pl.multiple_of(i * bs, bs), bs)
            for c in range(rows):
                dense[u, at_rows, c * bs : (c + 1) * bs] = raw[i, tab[u * rows + c, i]]
            return 0

        lax.fori_loop(0, rows, one, 0)

    size = rows * bs
    part_cols = []
    for n, width in enumerate(T_PARTS):
        start = sum(T_PARTS[:n]) * bs
        part_cols.append(slice(start, start + width * bs))
    pieces = [(slice(0, size), cols) for cols in part_cols[:-1]]
    pieces += [(slice(0, size // 2), part_cols[-1]), (slice(size // 2, size), part_cols[-1])]

    def target(kind, d):
        if kind < T_DIAG:
            return got.at[kind, d]
        at_rows, cols = pieces[kind - T_DIAG]
        return got.at[T_DIAG, d, at_rows, cols]

    def transfer(kind, d, source):
        return pltpu.make_async_remote_copy(
            src_ref=source,
            dst_ref=target(kind, d ^ 1),
            send_sem=send_sem.at[kind, d],
            recv_sem=recv_sem.at[kind, d ^ 1],
            device_id=neighbour(d),
            device_id_type=MESH,
        )

    def arrival(kind, d):
        return pltpu.make_async_remote_copy(
            src_ref=target(kind, d),
            dst_ref=target(kind, d),
            send_sem=send_sem.at[kind, d],
            recv_sem=recv_sem.at[kind, d],
            device_id=neighbour(d),
            device_id_type=MESH,
        )

    sends = []

    def send(kind, d, source):
        copy = transfer(kind, d, source)
        copy.start()
        sends.append(copy)

    copies[1].wait()
    densify(y_raw, y_own, 4)
    send(Y_EDGE, 3, y_own.at[4])
    for d in (0, 1):
        densify(y_raw, y_own, 1 + d)
        send(Y_EDGE, d, y_own.at[1 + d])
    densify(y_raw, y_own, 0)
    densify(y_raw, y_own, 3)
    for d in (3, 0, 1):
        send(Y_DIAG, d, y_own.at[0])
    pl.semaphore_wait(entered, 1)
    send(Y_EDGE, 2, y_own.at[3])
    send(Y_DIAG, 2, y_own.at[0])
    copies[2].wait()
    for d in SEND_ORDER:
        densify(z_raw, z_own, 1 + d)
        send(Z_EDGE, d, z_own.at[1 + d])
    densify(z_raw, z_own, 0)
    for d in SEND_ORDER:
        send(Z_DIAG, d, z_own.at[0])

    for u in range(9):
        for c in range(rows):
            for i in range(rows):
                keep[u, i : i + 1, c * bs : (c + 1) * bs] = jnp.full(
                    (1, bs), tab[u * rows + c, i], jnp.int32
                )

    def dot(a, b):
        return jnp.dot(a, b, preferred_element_type=jnp.float32)

    def store_t(target, u, diagonal):
        def one(i, _):
            at_rows = pl.ds(pl.multiple_of(i * bs, bs), bs)
            value = -0.5 * acc[at_rows, :]
            if diagonal:
                r = lax.broadcasted_iota(jnp.int32, value.shape, 0) + i * bs
                s = lax.broadcasted_iota(jnp.int32, value.shape, 1)
                value = jnp.where(r == s, 1.5 + value, value)
            present = jnp.broadcast_to(keep[u, pl.ds(i, 1), :], value.shape) < lanes
            target[at_rows, :] = jnp.where(present, value, 0.0).astype(jnp.bfloat16)
            return 0

        lax.fori_loop(0, rows, one, 0)

    def store_blocks(blocks, u, source):
        def one(i, _):
            at_rows = pl.ds(pl.multiple_of(i * bs, bs), bs)
            for c in range(rows):
                block = source[at_rows, c * bs : (c + 1) * bs]
                blocks[u * rows + c, i] = block.astype(jnp.bfloat16)
            return 0

        lax.fori_loop(0, rows, one, 0)

    acc[...] = dot(z_own[0], y_own[0])

    def add_edge(d, _):
        arrival(Y_EDGE, d).wait_recv()
        acc[...] += dot(z_own[1 + d], got[Y_EDGE, d])
        return 0

    lax.fori_loop(0, 4, add_edge, 0)
    store_t(t_own.at[0], 0, True)
    hops, forwards = [], []
    for p in range(2):
        kind = T_DIAG + T_KINDS - 2 + p
        hops.append(
            pltpu.make_async_remote_copy(
                src_ref=t_own.at[0, pieces[kind - T_DIAG][0], pieces[kind - T_DIAG][1]],
                dst_ref=relay_buf.at[p],
                send_sem=send_sem.at[kind, 3],
                recv_sem=relay_sem.at[p, 0],
                device_id=relay_place,
                device_id_type=MESH,
            )
        )
        forwards.append(
            pltpu.make_async_remote_copy(
                src_ref=relay_buf.at[p],
                dst_ref=target(kind, 2),
                send_sem=relay_sem.at[p, 1],
                recv_sem=recv_sem.at[kind, 2],
                device_id=end_place,
                device_id_type=MESH,
            )
        )
    for n in range(T_KINDS):
        p = n - (T_KINDS - 2)
        for d in SEND_ORDER:
            source = t_own.at[0, pieces[n][0], pieces[n][1]]
            if p >= 0 and d == 3:
                direct = transfer(T_DIAG + n, d, source)
                pl.when(detours[p])(hops[p].start)
                pl.when(jnp.logical_not(detours[p]))(direct.start)
                sends.append(direct)
            else:
                send(T_DIAG + n, d, source)
    y_acc[...] = dot(y_own[0], t_own[0])
    z_acc[...] = dot(t_own[0], z_own[0])

    def t_edge(d, _):
        acc[...] = dot(z_own[0], y_own[1 + d])
        arrival(Y_DIAG, d).wait_recv()
        acc[...] += dot(z_own[1 + d], got[Y_DIAG, d])
        store_t(t_own.at[1 + d], 1 + d, False)
        y_part[d] = dot(y_own[0], t_own[1 + d])
        return 0

    lax.fori_loop(0, 4, t_edge, 0)

    def pass_on(p):
        hops[p].wait_recv()
        forwards[p].start()

    for p in range(2):
        pl.when(relays[p])(functools.partial(pass_on, p))

    def z_step(d, _):
        arrival(Z_EDGE, d).wait_recv()
        acc[...] = dot(got[Z_EDGE, d], y_own[0])
        z_acc[...] += dot(t_own[1 + d], got[Z_EDGE, d])
        arrival(Z_DIAG, d).wait_recv()
        acc[...] += dot(got[Z_DIAG, d], got[Y_EDGE, d])
        store_t(t_near, 5 + d, False)
        y_acc[...] += dot(y_own[1 + d], t_near[...])
        acc[...] = dot(t_own[0], z_own[1 + d])
        acc[...] += dot(t_own[1 + d], got[Z_DIAG, d])
        store_blocks(z_dense, 1 + d, acc)
        return 0

    lax.fori_loop(0, 4, z_step, 0)
    store_blocks(z_dense, 0, z_acc)
    store_blocks(y_dense, 0, y_acc)

    def gather(blocks, out):
        def one(i, _):
            for m in range(lanes):
                out[i, m] = blocks[tab[at_back + m, i], i]
            return 0

        lax.fori_loop(0, rows, one, 0)

    gather(z_dense, z_out)

    for n, width in enumerate(T_PARTS):
        cols = part_cols[n]

        def y_step(d, _):
            arrival(T_DIAG + n, d).wait_recv()
            if n == len(T_PARTS) - 1:
                arrival(T_DIAG + n + 1, d).wait_recv()
            part = dot(y_own[1 + d], got[T_DIAG, d, :, cols]) + y_part[d, :, cols]
            part = part.astype(jnp.bfloat16)
            for i in range(rows):
                for c in range(width):
                    q = (1 + d) * rows + sum(T_PARTS[:n]) + c
                    y_dense[q, i] = part[i * bs : (i + 1) * bs, c * bs : (c + 1) * bs]
            return 0

        lax.fori_loop(0, 4, y_step, 0)
    gather(y_dense, y_out)
    for copy in sends:
        copy.wait_send()
    for p in range(2):
        pl.when(relays[p])(forwards[p].wait_send)


def write_kernel(y_vmem, z_vmem, y_out, z_out, sem):
    copies = []
    for n, (source, target) in enumerate(((z_vmem, z_out), (y_vmem, y_out))):
        copies.append(pltpu.make_async_copy(source, target, sem.at[n, 0]))
    for copy in copies:
        copy.start()
    for copy in copies:
        copy.wait()


def on_device(row_count, col_count, y_blocks, z_blocks, pattern):
    rows, lanes, bs, _ = y_blocks.shape
    size = rows * bs
    bf16, f32 = jnp.bfloat16, jnp.float32
    unit = (size, size)
    held = pltpu.VMEM(y_blocks.shape, bf16)
    out = jax.ShapeDtypeStruct(y_blocks.shape, bf16)
    any_space = pl.BlockSpec(memory_space=pl.ANY)
    vmem = pl.BlockSpec(memory_space=pltpu.VMEM)
    y_vmem, z_vmem = pl.pallas_call(
        functools.partial(step_kernel, (row_count, col_count, rows, bs)),
        out_shape=(held, held),
        in_specs=[any_space, any_space, any_space],
        out_specs=(vmem, vmem),
        scratch_shapes=[
            pltpu.VMEM((rows, lanes + 1, bs, bs), bf16),
            pltpu.VMEM((rows, lanes + 1, bs, bs), bf16),
            pltpu.VMEM((lanes, pattern.shape[0]), jnp.int32),
            pltpu.VMEM((9, rows, size), jnp.int32),
            pltpu.VMEM((9 * rows + lanes, 128), jnp.int32),
            pltpu.SMEM((9 * rows + lanes, 128), jnp.int32),
            pltpu.VMEM((5,) + unit, bf16),
            pltpu.VMEM((5,) + unit, bf16),
            pltpu.VMEM((5,) + unit, bf16),
            pltpu.VMEM((5, 4) + unit, bf16),
            pltpu.VMEM(unit, bf16),
            pltpu.VMEM((4,) + unit, f32),
            pltpu.VMEM(unit, f32),
            pltpu.VMEM(unit, f32),
            pltpu.VMEM(unit, f32),
            pltpu.VMEM((5 * rows, rows, bs, bs), bf16),
            pltpu.VMEM((5 * rows, rows, bs, bs), bf16),
            pltpu.VMEM((2, size // 2, T_PARTS[-1] * bs), bf16),
            pltpu.SemaphoreType.DMA((4,)),
            pltpu.SemaphoreType.DMA((4 + T_KINDS, 4)),
            pltpu.SemaphoreType.DMA((4 + T_KINDS, 4)),
            pltpu.SemaphoreType.DMA((2, 2)),
            pltpu.SemaphoreType.REGULAR,
        ],
        compiler_params=pltpu.CompilerParams(
            collective_id=0, has_side_effects=True, vmem_limit_bytes=48 << 20
        ),
    )(y_blocks, z_blocks, pltpu.with_memory_space_constraint(pattern.T, pltpu.HBM))
    return pl.pallas_call(
        write_kernel,
        out_shape=(out, out),
        in_specs=[vmem, vmem],
        out_specs=(any_space, any_space),
        scratch_shapes=[pltpu.SemaphoreType.DMA((2, rows))],
        compiler_params=pltpu.CompilerParams(vmem_limit_bytes=1 << 20),
    )(
        pltpu.with_memory_space_constraint(y_vmem, pltpu.VMEM),
        pltpu.with_memory_space_constraint(z_vmem, pltpu.VMEM),
    )


def solution(mesh):
    spec = P(("row", "col"), None, None, None)
    return jax.shard_map(
        functools.partial(on_device, mesh.shape["row"], mesh.shape["col"]),
        mesh=mesh,
        in_specs=(spec, spec, P()),
        out_specs=(spec, spec),
        check_vma=False,
    )
```
